32 devices in a mesh: groups: 2 (over y), tm: 4 (over z), rec: 2 (over x), mp: 2 (over core).
Axes of the slice: x: 2, y: 2, z: 4, core: 2. Of those that a mesh axis runs over, the one named last changes fastest.
Arguments:
- frames: bfloat16 [8, 4096, 512], P(('groups', 'rec'), 'tm'), parts along dimension 0, may hold values from -6 to 6
- lengths: int32 [8], P(('groups', 'rec')), parts along dimension 0, may hold values from 1024 to 4096
- memory_in: bfloat16 [8, 64, 512], P(('groups', 'rec'), 'tm'), parts along dimension 0, may hold values from -6 to 6
- gain_attn: float32 [512], replicated, may hold values from 0.25 to 1.75
- w_query: bfloat16 [512, 512], P(None, 'mp')
- w_key: bfloat16 [512, 512], P(None, 'mp')
- w_value: bfloat16 [512, 512], P(None, 'mp'), may hold values from -0.25 to 0.25
- w_out: bfloat16 [512, 512], P('mp'), may hold values from -0.25 to 0.25
- gain_conv: float32 [512], replicated, may hold values from 0.25 to 1.75
- w_conv_in: bfloat16 [2, 512, 512], P(None, None, 'mp'), may hold values from -0.25 to 0.25
- w_depth: bfloat16 [31, 512], P(None, 'mp'), may hold values from -1 to 1
- w_conv_out: bfloat16 [512, 512], P('mp'), may hold values from -0.25 to 0.25
- gain_ffn: float32 [512], replicated, may hold values from 0.25 to 1.75
- w_ffn_in: bfloat16 [512, 2048], P(None, 'mp'), may hold values from -0.25 to 0.25
- w_ffn_out: bfloat16 [512, 2048], P(None, 'mp'), may hold values from -0.125 to 0.125
Outputs:
- output: bfloat16 [8, 4096, 512], P(('groups', 'rec'), ('tm', 'mp')), parts along dimension 0
- memory_out: bfloat16 [8, 64, 512], P(('groups', 'rec'), 'tm'), parts along dimension 0
The draws below stay inside these ranges and needn't reach their ends.
There are 2 independent parts, one for each index of `groups`. The reference program is written for one: setup_inputs(seed, part) draws one part's arguments, and reference() takes and returns one part's arrays. A program takes and returns all parts, laid end to end along the dimension named above; an argument that names none is the same for every part. Nothing has to cross between parts.
Inputs may be any that keep to these rules, and one draw needn't show every extreme that they name: `lengths`: the number of valid frames of each recording; its frames from that index on are padding.
All inputs are finite; a program needn't handle non-finite values.
Results may differ from the reference program's by a relative error of at most 0.023.
Values may be sent and summed in bfloat16 or wider, within the bound.
No kernel may reach another device: no remote copies, remote signals or barrier semaphores. Data moves between devices by JAX's collectives and lax.ppermute only.
A program may use at most 128 MiB of HBM per device.

```python
import jax
import jax.numpy as jnp
from jax import lax

D = 512
HEADS = 8
FF = 2048
CK = 31
SEG = 64
LEFT = 32
LOOK = 16
DH = 64
REC = 4
FR = 4096
SEGS = 64


def query_key_base(key):
    base_matrix = jax.random.truncated_normal(jax.random.fold_in(key, 101), -4.0, 4.0, (D, D), jnp.float32)
    return base_matrix * D ** (-0.5)


def draw_w_query(key, part):
    base_matrix = query_key_base(key)
    return base_matrix.astype(jnp.bfloat16)


def draw_w_key(key, part):
    other_matrix = jax.random.truncated_normal(jax.random.fold_in(key, 103), -4.0, 4.0, (D, D), jnp.float32) * D ** (-0.5)
    return other_matrix.astype(jnp.bfloat16)


def plant(array, key, least, largest):
    dims = array.shape
    place = [jax.random.randint(jax.random.fold_in(key, axis), (), 0, dims[axis]) for axis in range(len(dims))]
    array = array.at[tuple(place)].set(least)
    longest = dims.index(max(dims))
    place[longest] = (place[longest] + 1) % dims[longest]
    return array.at[tuple(place)].set(largest)


def level_of(stream_key, shape, shards, smallest, top_value):
    def one(axis_at, parts):
        steps = jax.random.uniform(jax.random.fold_in(jax.random.fold_in(stream_key, 6), axis_at), (parts,), jnp.float32, smallest / len(shards), top_value / len(shards))
        return jnp.repeat(jnp.exp(steps), shape[axis_at] // parts).reshape((-1,) + (1,) * (len(shape) - axis_at - 1))

    gain = one(*shards[0])
    for cut in shards[1:]:
        gain = gain * one(*cut)
    return gain


def noise(stream_key, dims, deviation, bound, pieces=(), kind=jnp.bfloat16):
    factor_of = level_of(stream_key, dims, pieces, -0.22, 0.18) if pieces else 1.0
    values = jax.random.normal(stream_key, dims, jnp.float32) * deviation * factor_of
    return jnp.minimum(jnp.maximum(values, -bound), bound).astype(kind)


def setup_inputs(seed: int = 0, part: int = 0) -> dict:
    key_list = jax.random.split(jax.random.key(seed), 16)
    part_splits = jax.random.split(jax.random.fold_in(key_list[15], part), 16)
    frames = noise(part_splits[0], (REC, FR, D), 1.0, 6.0, ((0, 2), (1, 4)))
    lengths = plant(jax.random.randint(part_splits[1], (REC,), FR // 4, FR + 1), jax.random.fold_in(part_splits[1], 1), FR // 4, FR).astype(jnp.int32)
    memory_in = noise(part_splits[2], (REC, SEGS, D), 1.0, 6.0, ((0, 2), (1, 4)))
    gain_attn = jnp.clip(1.0 + 0.15 * jax.random.normal(key_list[3], (D,), jnp.float32), 0.25, 1.75)
    w_query = draw_w_query(jax.random.fold_in(key_list[15], 71), part)
    w_key = draw_w_key(jax.random.fold_in(key_list[15], 71), part)
    w_value = noise(key_list[6], (D, D), D ** -0.5, 0.25, ((1, 2),))
    w_out = noise(key_list[7], (D, D), D ** -0.5, 0.25, ((0, 2),))
    gain_conv = jnp.clip(1.0 + 0.15 * jax.random.normal(key_list[8], (D,), jnp.float32), 0.25, 1.75)
    w_conv_in = noise(key_list[9], (2, D, D), D ** -0.5, 0.25, ((2, 2),))
    w_depth = noise(key_list[10], (CK, D), CK ** -0.5, 1.0, ((1, 2),))
    w_conv_out = noise(key_list[11], (D, D), D ** -0.5, 0.25, ((0, 2),))
    gain_ffn = jnp.clip(1.0 + 0.15 * jax.random.normal(key_list[12], (D,), jnp.float32), 0.25, 1.75)
    w_ffn_in = noise(key_list[13], (D, FF), D ** -0.5, 0.25, ((1, 2),))
    w_ffn_out = noise(key_list[14], (D, FF), FF ** -0.5, 0.125, ((1, 2),))
    return dict(frames=frames, lengths=lengths, memory_in=memory_in, gain_attn=gain_attn, w_query=w_query, w_key=w_key, w_value=w_value, w_out=w_out, gain_conv=gain_conv, w_conv_in=w_conv_in, w_depth=w_depth, w_conv_out=w_conv_out, gain_ffn=gain_ffn, w_ffn_in=w_ffn_in, w_ffn_out=w_ffn_out)


EPSILON = 1e-05
NEGATIVE_FILL = -1e+30

def layer_norm(inputs, gain_vec):
    inputs = inputs.astype(jnp.float32)
    average = lax.optimization_barrier(jnp.mean(inputs, axis=-1, keepdims=True))
    centred = inputs - average
    spread = lax.optimization_barrier(jnp.mean(centred * centred, axis=-1, keepdims=True))
    return centred * lax.rsqrt(spread + EPSILON) * gain_vec

def project(inputs, weight):
    return jnp.dot(inputs, weight, preferred_element_type=jnp.float32).astype(jnp.bfloat16)

def padded_total_length(probs):
    return lax.optimization_barrier(probs.astype(jnp.bfloat16)).astype(jnp.float32)

def windows(matrix):
    columns = matrix.shape[1]
    padded = jnp.concatenate([jnp.zeros((LEFT, columns), matrix.dtype), matrix, jnp.zeros((SEG - LEFT, columns), matrix.dtype)], axis=0)
    first_block = padded[:FR].reshape(SEGS, SEG, columns)
    second_block = padded[SEG:].reshape(SEGS, SEG, columns)
    joined = jnp.concatenate([first_block, second_block], axis=1)
    return joined.reshape(SEGS, 2 * SEG, HEADS, DH).astype(jnp.float32)

def utterance_entry(frames, bank, length, weights):
    gain_attn, w_query, w_key, w_value, w_out, gain_conv, w_conv_in, w_depth, w_conv_out, gain_ffn, w_ffn_in, w_ffn_out = weights
    frame_index = jnp.arange(FR, dtype=jnp.int32)
    valid_mask = frame_index < length
    normed = layer_norm(frames, gain_attn).astype(jnp.bfloat16)
    queries = project(normed, w_query)
    key_rows = project(normed, w_key)
    value_rows = project(normed, w_value)
    bank_keys = project(bank, w_key)
    bank_values = project(bank, w_value)
    summary = lax.optimization_barrier(jnp.mean(normed.astype(jnp.float32).reshape(SEGS, SEG, D), axis=1)).astype(jnp.bfloat16)
    summary_query = project(summary, w_query)
    window_keys = windows(key_rows)
    span_payload_vectors = windows(value_rows)
    window_offsets = jnp.arange(2 * SEG, dtype=jnp.int32)
    seg_index = jnp.arange(SEGS, dtype=jnp.int32)
    win_pos = seg_index[:, None] * SEG - LEFT + window_offsets[None, :]
    window_valid_mask = (window_offsets[None, :] < LEFT + SEG + LOOK) & (win_pos >= 0) & (win_pos < length)
    bank_live = seg_index * SEG < length
    mem_ok = bank_live[:, None] & (seg_index[:, None] < (frame_index // SEG)[None, :])
    summary_valid_mask = bank_live[None, :] & (seg_index[None, :] < seg_index[:, None])
    score_scaling = DH ** (-0.5)
    query_heads = queries.astype(jnp.float32).reshape(SEGS, SEG, HEADS, DH)
    memory_bank_key_heads = bank_keys.astype(jnp.float32).reshape(SEGS, HEADS, DH)
    stored_slot_payload_per_attender = bank_values.astype(jnp.float32).reshape(SEGS, HEADS, DH)
    win_scores = jnp.einsum('mqhd,mkhd->mhqk', query_heads, window_keys) * score_scaling
    win_scores = jnp.where(window_valid_mask[:, None, None, :], win_scores, NEGATIVE_FILL)
    mem_scores = jnp.einsum('fhd,jhd->hjf', queries.astype(jnp.float32).reshape(FR, HEADS, DH), memory_bank_key_heads) * score_scaling
    mem_scores = jnp.where(mem_ok[None], mem_scores, NEGATIVE_FILL)
    mem_top = lax.optimization_barrier(jnp.max(mem_scores, axis=1)).reshape(HEADS, SEGS, SEG).transpose(1, 0, 2)
    row_top = jnp.maximum(lax.optimization_barrier(jnp.max(win_scores, axis=-1)), mem_top)
    win_probs = jnp.exp(win_scores - row_top[..., None])
    mem_probs = jnp.exp(mem_scores - row_top.transpose(1, 0, 2).reshape(HEADS, FR)[:, None, :])
    row_total = lax.optimization_barrier(jnp.sum(win_probs, axis=-1)) + lax.optimization_barrier(jnp.sum(mem_probs, axis=1)).reshape(HEADS, SEGS, SEG).transpose(1, 0, 2)
    near_part = jnp.einsum('mhqk,mkhd->mqhd', padded_total_length(win_probs), span_payload_vectors)
    far_part = jnp.einsum('hjf,jhd->fhd', padded_total_length(mem_probs), stored_slot_payload_per_attender).reshape(SEGS, SEG, HEADS, DH)
    context = ((near_part + far_part) / row_total.transpose(0, 2, 1)[..., None]).astype(jnp.bfloat16).reshape(FR, D)
    summary_query_heads = summary_query.astype(jnp.float32).reshape(SEGS, HEADS, DH)
    summary_window_scores = jnp.where(window_valid_mask[:, None, :], jnp.einsum('zfq,zwfq->zfw', summary_query_heads, window_keys) * score_scaling, NEGATIVE_FILL)
    summary_memory_scores = jnp.where(summary_valid_mask[:, None, :], jnp.einsum('enu,wnu->enw', summary_query_heads, memory_bank_key_heads) * score_scaling, NEGATIVE_FILL)
    sum_top = jnp.maximum(lax.optimization_barrier(jnp.max(summary_window_scores, axis=-1)), lax.optimization_barrier(jnp.max(summary_memory_scores, axis=-1)))
    digest_span_attention_weights = jnp.exp(summary_window_scores - sum_top[..., None])
    digest_slot_attention_weights = jnp.exp(summary_memory_scores - sum_top[..., None])
    sum_total = lax.optimization_barrier(jnp.sum(digest_span_attention_weights, axis=-1)) + lax.optimization_barrier(jnp.sum(digest_slot_attention_weights, axis=-1))
    digest_span_lines = jnp.einsum('vzd,vdzs->vzs', padded_total_length(digest_span_attention_weights), span_payload_vectors) + jnp.einsum('ljt,tju->lju', padded_total_length(digest_slot_attention_weights), stored_slot_payload_per_attender)
    summary_context = (digest_span_lines / sum_total[..., None]).astype(jnp.bfloat16).reshape(SEGS, D)
    first_sum = frames.astype(jnp.float32) + jnp.dot(context, w_out, preferred_element_type=jnp.float32)
    memory_out = jnp.where(bank_live[:, None], jnp.dot(summary_context, w_out, preferred_element_type=jnp.float32), 0.0).astype(jnp.bfloat16)
    conv_input = jnp.where(valid_mask[:, None], layer_norm(first_sum, gain_conv), 0.0).astype(jnp.bfloat16)
    lin_part = jnp.dot(conv_input, w_conv_in[0], preferred_element_type=jnp.float32)
    gate_part = jnp.dot(conv_input, w_conv_in[1], preferred_element_type=jnp.float32)
    glu = (lin_part * jax.nn.sigmoid(gate_part)).astype(jnp.bfloat16)
    padded_glu = jnp.concatenate([jnp.zeros((CK - 1, D), jnp.bfloat16), glu], axis=0).astype(jnp.float32)
    taps = w_depth.astype(jnp.float32)
    depthwise = jnp.zeros((FR, D), jnp.float32)
    for tap_index in range(CK):
        depthwise = depthwise + taps[tap_index][None, :] * padded_glu[tap_index:tap_index + FR]
    activated = jax.nn.silu(depthwise).astype(jnp.bfloat16)
    second_sum = first_sum + jnp.dot(activated, w_conv_out, preferred_element_type=jnp.float32)
    ffn_input = layer_norm(second_sum, gain_ffn).astype(jnp.bfloat16)
    hidden = jax.nn.silu(jnp.dot(ffn_input, w_ffn_in, preferred_element_type=jnp.float32)).astype(jnp.bfloat16)
    third_sum = second_sum + lax.dot_general(hidden, w_ffn_out, (((1,), (1,)), ((), ())), preferred_element_type=jnp.float32)
    output = jnp.where(valid_mask[:, None], third_sum, 0.0).astype(jnp.bfloat16)
    return (output, memory_out)

def reference(frames, lengths, memory_in, gain_attn, w_query, w_key, w_value, w_out, gain_conv, w_conv_in, w_depth, w_conv_out, gain_ffn, w_ffn_in, w_ffn_out):
    weights = (gain_attn, w_query, w_key, w_value, w_out, gain_conv, w_conv_in, w_depth, w_conv_out, gain_ffn, w_ffn_in, w_ffn_out)

    def per_recording(record):
        return utterance_entry(record[0], record[1], record[2], weights)
    output, memory_out = lax.map(per_recording, (frames, memory_in, lengths))
    return (output, memory_out)
```

```python
import functools

import jax
import jax.numpy as jnp
from jax import lax
from jax.experimental import pallas as pl
from jax.experimental.pallas import tpu as pltpu
from jax.sharding import PartitionSpec as P


CK = 31
SEG = 64
LEFT = 32
LOOK = 16
DH = 64
EPSILON = 1e-05
NEGATIVE_FILL = -1e30

HALO = LEFT + SEG
CONV = 32
WINDOW = 2 * SEG + LEFT + LOOK

BF16 = jnp.bfloat16
F32 = jnp.float32


def norm_rows(rows, gain):
    average = jnp.mean(rows, axis=-1, keepdims=True)
    centred = rows - average
    spread = jnp.mean(centred * centred, axis=-1, keepdims=True)
    return centred * lax.rsqrt(spread + EPSILON) * gain


def dot(a, b):
    return jnp.dot(a, b, preferred_element_type=F32)


def dot_nt(a, b):
    return lax.dot_general(a, b, (((1,), (1,)), ((), ())), preferred_element_type=F32)


def gated(half_value, half_gate):
    return half_value + half_value * jnp.tanh(half_gate)


def load_around(rec, frames, halo, target, core, own, before, after, sems):
    def edges(side):
        if side == 0:
            pieces = [(halo, HALO - before, 0, before), (frames, own, before + own, after)]
        else:
            pieces = [(frames, own - before, 0, before), (halo, 0, before + own, after)]
        return [
            pltpu.make_async_copy(
                source.at[rec, pl.ds(at, size)], target.at[rec, pl.ds(to, size)], sems.at[1 + place]
            )
            for place, (source, at, to, size) in enumerate(pieces)
            if size
        ]

    body = pltpu.make_async_copy(
        frames.at[rec, pl.ds(pl.multiple_of(core * own, own), own)],
        target.at[rec, pl.ds(before, own)],
        sems.at[0],
    )

    def start():
        body.start()
        for side in range(2):

            @pl.when(core == side)
            def _():
                for copy in edges(side):
                    copy.start()

    def wait():
        body.wait()
        for side in range(2):

            @pl.when(core == side)
            def _():
                for copy in edges(side):
                    copy.wait()

    return start, wait


def attention_kernel(*refs, seg_block, blocks):
    lengths, frames, halo = refs[0:3]
    memory = refs[3 : 3 + blocks]
    weights = refs[3 + blocks : 11 + blocks]
    gain_attn = refs[11 + blocks]
    ctx_out, memory_out = refs[12 + blocks : 14 + blocks]
    (
        x_s,
        n_s,
        q_s,
        k_s,
        v_s,
        m_s,
        kb_s,
        vb_s,
        sq_s,
        ctx_s,
        sctx_s,
        bias_s,
        kcat_s,
        vcat_s,
        w_s,
        wa_s,
        sems,
        m_sems,
        w_sems,
        o_sems,
    ) = refs[14 + blocks :]
    rec_count, ext, width = x_s.shape
    own = ext - HALO - LOOK
    frame_count = frames.shape[1]
    bank = seg_block * blocks
    keys = kcat_s.shape[1]
    half = width // 2
    block = lax.axis_index("tm")
    core = lax.axis_index("mp")
    start = block * frame_count + core * own
    pairs = own // (2 * SEG)
    group_rows = 2 * SEG

    loads = [
        load_around(rec, frames, halo, x_s, core, own, HALO, LOOK, sems.at[rec])
        for rec in range(rec_count)
    ]
    loads[0][0]()
    memory_copies = [
        pltpu.make_async_copy(
            memory[at], m_s.at[:, pl.ds(at * seg_block, seg_block)], m_sems.at[at]
        )
        for at in range(blocks)
    ]
    targets = [w_s.at[at] for at in range(6)] + [wa_s.at[0], wa_s.at[1]]
    copies = [
        pltpu.make_async_copy(source, target, w_sems.at[at])
        for at, (source, target) in enumerate(zip(weights, targets))
    ]
    weight_copies, out_copies = copies[0:6], copies[6:8]
    for copy in weight_copies:
        copy.start()
    for load in loads[1:]:
        load[0]()
    for copy in memory_copies + out_copies:
        copy.start()
    kcat_s[...] = jnp.zeros_like(kcat_s)
    vcat_s[:, :, :, 0:128] = jnp.zeros(vcat_s.shape[0:3] + (128,), BF16)
    vcat_s[:, :, :, 128:256] = jnp.ones(vcat_s.shape[0:3] + (128,), BF16)
    wq_o, wq_p, wk_o, wk_p, wv_o, wv_p = [w_s.at[at] for at in range(6)]
    chunks = 3
    step = ext // chunks
    for rec in range(rec_count):
        loads[rec][1]()
        if rec == 0:
            for copy in weight_copies:
                copy.wait()
        for part in range(chunks):
            rows = pl.ds(part * step, step)
            normed = norm_rows(x_s[rec, rows, :].astype(F32), gain_attn[...]).astype(BF16)
            n_s[rec, rows, :] = normed
            for side, (wq, wk, wv) in enumerate(((wq_o, wk_o, wv_o), (wq_p, wk_p, wv_p))):
                cols = pl.ds(side * half, half)
                q_s[rec, rows, cols] = (dot(normed, wq[...]) * DH**-0.5).astype(BF16)
                k_s[rec, rows, cols] = dot(normed, wk[...]).astype(BF16)
                v_s[rec, rows, cols] = dot(normed, wv[...]).astype(BF16)

    mean_rows = pairs * 16
    row_id = lax.broadcasted_iota(jnp.int32, (mean_rows, own), 0)
    col_id = lax.broadcasted_iota(jnp.int32, (mean_rows, own), 1)
    seg_of_row = jnp.where((row_id & 15) < 2, (row_id >> 4) * 2 + (row_id & 15), -1)
    averaging = jnp.where(seg_of_row == (col_id >> 6), 1.0 / SEG, 0.0).astype(BF16)
    summary = jnp.concatenate(
        [dot(averaging, n_s[rec, HALO : HALO + own, :]).astype(BF16) for rec in range(rec_count)],
        axis=0,
    )
    for copy in memory_copies:
        copy.wait()
    bank_rows = m_s[...].reshape(rec_count * bank, width)
    for part, (wq, wk, wv) in enumerate(((wq_o, wk_o, wv_o), (wq_p, wk_p, wv_p))):
        cols = pl.ds(part * half, half)
        kb_s[:, :, cols] = dot(bank_rows, wk[...]).astype(BF16).reshape(rec_count, bank, half)
        vb_s[:, :, cols] = dot(bank_rows, wv[...]).astype(BF16).reshape(rec_count, bank, half)
        sq_s[:, cols] = (dot(summary, wq[...]) * DH**-0.5).astype(BF16)

    lane = lax.broadcasted_iota(jnp.int32, (1, 128), 1)
    left_head = lane < DH

    def attend(place, rec, base, row_count, rows_padded, seg_first, load_queries, store):
        r_id = lax.broadcasted_iota(jnp.int32, (row_count, keys), 0)
        l_id = lax.broadcasted_iota(jnp.int32, (row_count, keys), 1)
        local = jnp.where(r_id < group_rows, r_id >> 6, r_id & 1)
        length = lengths[rec]
        position = start - HALO + base + l_id
        low = local * SEG
        in_window = (
            (l_id >= low)
            & (l_id < low + LEFT + SEG + LOOK)
            & (position >= 0)
            & (position < length)
            & (l_id < WINDOW)
        )
        slot_at = l_id - WINDOW
        slot = slot_at ^ (block * seg_block)
        in_bank = (
            (slot_at >= 0)
            & (slot_at < bank)
            & (slot < seg_first + local)
            & (slot * SEG < length)
        )
        bias_s[place, 0:row_count, :] = jnp.where(in_window | in_bank, 0.0, NEGATIVE_FILL)

        def scores_of(pair):
            cols = pl.ds(pair * 128, 128)
            kcat_s[place, 0:WINDOW, cols] = k_s[rec, pl.ds(pl.multiple_of(base, 16), WINDOW), cols]
            kcat_s[place, WINDOW : WINDOW + bank, cols] = kb_s[rec, :, cols]
            vcat_s[place, pair, 0:WINDOW, 0:128] = v_s[
                rec, pl.ds(pl.multiple_of(base, 16), WINDOW), cols
            ]
            vcat_s[place, pair, WINDOW : WINDOW + bank, 0:128] = vb_s[rec, :, cols]
            query = load_queries(cols)
            zero = jnp.zeros_like(query)
            both = jnp.concatenate(
                [jnp.where(left_head, query, zero), jnp.where(left_head, zero, query)], axis=0
            )
            return dot_nt(both, kcat_s[place, :, cols])

        def probs_of(scores):
            probs = []
            for side in range(2):
                part = scores[side * rows_padded : side * rows_padded + row_count]
                part = part + bias_s[place, 0:row_count, :]
                part = jnp.exp(part - jnp.max(part, axis=1, keepdims=True))
                part = part.astype(BF16)
                if rows_padded > row_count:
                    part = jnp.concatenate(
                        [part, jnp.zeros((rows_padded - row_count, keys), BF16)], axis=0
                    )
                probs.append(part)
            return jnp.concatenate(probs, axis=0)

        def mix(pair, probs):
            mixed = dot(probs, vcat_s[place, pair])
            sides = [
                mixed[side * rows_padded : side * rows_padded + row_count] for side in range(2)
            ]
            value = jnp.where(
                left_head,
                sides[0][:, 0:128] / sides[0][:, 128:256],
                sides[1][:, 0:128] / sides[1][:, 128:256],
            )
            store(pl.ds(pair * 128, 128), value)

        pair_count = width // 128
        scores = scores_of(0)
        for pair in range(pair_count):
            following = scores_of(pair + 1) if pair + 1 < pair_count else None
            mix(pair, probs_of(scores))
            scores = following

    def pair_of_segments(place, rec, pair):
        base = HALO - LEFT + pair * group_rows

        def load_queries(cols):
            return jnp.concatenate(
                [
                    q_s[rec, pl.ds(pl.multiple_of(base + LEFT, 16), group_rows), cols],
                    sq_s[pl.ds(pl.multiple_of((rec * pairs + pair) * 16, 16), 16), cols],
                ],
                axis=0,
            )

        def store(cols, value):
            ctx_s[rec, pl.ds(pl.multiple_of(CONV + pair * group_rows, 16), group_rows), cols] = (
                value[0:group_rows].astype(BF16)
            )
            sctx_s[rec, pl.ds(pl.multiple_of(pair * 8, 8), 8), cols] = value[group_rows:]

        attend(
            place,
            rec,
            base,
            group_rows + 8,
            group_rows + 16,
            start // SEG + 2 * pair,
            load_queries,
            store,
        )

    def segment_before(place, rec):
        def load_queries(cols):
            return q_s[rec, HALO - CONV : HALO, cols]

        def store(cols, value):
            ctx_s[rec, 0:CONV, cols] = value.astype(BF16)

        attend(place, rec, 0, CONV, CONV, start // SEG - 1, load_queries, store)

    ctx_copies = [
        pltpu.make_async_copy(ctx_s.at[rec], ctx_out.at[rec], o_sems.at[rec])
        for rec in range(rec_count)
    ]
    for rec in range(rec_count):
        segment_before(rec % 2, rec)
    for rec in range(rec_count):

        @pl.loop(0, pairs // 2)
        def _(index):
            for place in range(2):
                pair_of_segments(place, rec, 2 * index + place)

        ctx_copies[rec].start()

    for copy in out_copies:
        copy.wait()
    summed = sctx_s[...].reshape(rec_count * pairs * 8, width).astype(BF16)
    vectors = dot(summed[:, 0:half], wa_s[0]) + dot(summed[:, half:width], wa_s[1])
    memory_out[...] = jnp.zeros_like(memory_out)
    segs = 2 * pairs
    for side in range(2):

        @pl.when(core == side)
        def _():
            for rec in range(rec_count):
                rows = [
                    jnp.where(
                        start + seg * SEG < lengths[rec],
                        vectors[rec * pairs * 8 + seg // 2 * 8 + seg % 2 :][0:1],
                        0.0,
                    )
                    for seg in range(segs)
                ]
                memory_out[rec, side * segs : (side + 1) * segs, :] = jnp.concatenate(
                    rows, axis=0
                ).astype(BF16)

    for copy in ctx_copies:
        copy.wait()


def convolution_kernel(
    lengths,
    frames,
    halo,
    ctx,
    wa_o,
    wa_p,
    wc_o,
    wc_p,
    wd_o,
    wd_p,
    wo_o,
    wo_p,
    wi_o,
    wi_p,
    wf_o,
    wf_p,
    gain_conv,
    gain_ffn,
    out,
    x_s,
    ctx_s,
    first_s,
    glu_s,
    g_s,
    act_s,
    fin_s,
    second_s,
    hid_s,
    out_s,
    wa_s,
    wc_s,
    wd_s,
    wo_s,
    wi_s,
    wf_s,
    sems,
    w_sems,
    o_sems,
):
    rec_count, ext, width = x_s.shape
    own = ext - CONV
    half = width // 2
    core = lax.axis_index("mp")
    start = lax.axis_index("tm") * frames.shape[1] + core * own

    loads = [
        load_around(rec, frames, halo, x_s, core, own, CONV, 0, sems.at[rec])
        for rec in range(rec_count)
    ]
    ctx_copies = [
        pltpu.make_async_copy(ctx.at[rec], ctx_s.at[rec], sems.at[rec, 3])
        for rec in range(rec_count)
    ]
    pairs_of = []
    for target, sides in ((wa_s, (wa_o, wa_p)), (wc_s, (wc_o, wc_p)), (wo_s, (wo_o, wo_p))):
        pairs_of += [(sides[0], target.at[0]), (sides[1], target.at[1])]
    for tile in range(width // 128):
        cols = pl.ds(tile * 128 % half, 128)
        pairs_of.append(((wd_o, wd_p)[tile * 128 // half].at[:, cols], wd_s.at[tile]))
    tiles = wi_s.shape[0] // 2
    for target, sides in ((wi_s, (wi_o, wi_p)), (wf_s, (wf_o, wf_p))):
        for side in range(2):
            for tile in range(tiles):
                pairs_of.append(
                    (sides[side].at[:, pl.ds(tile * 256, 256)], target.at[side * tiles + tile])
                )
    copies = [
        pltpu.make_async_copy(source, target, w_sems.at[at])
        for at, (source, target) in enumerate(pairs_of)
    ]
    ctx_copies[0].start()
    for copy in copies[0:2]:
        copy.start()
    loads[0][0]()
    for copy in copies[2:4]:
        copy.start()
    ctx_copies[0].wait()
    loads[0][1]()
    for copy in copies[0:2]:
        copy.wait()
    mid_copies, conv_copies = copies[4:6], copies[6 : 6 + width // 128]
    late_copies = copies[6 + width // 128 :]

    def gated_frames(rec, at, size):
        rows = pl.ds(at if isinstance(at, int) else pl.multiple_of(at, 16), size)
        held = {}

        def project():
            context = ctx_s[rec, rows, :]
            term = dot(context[:, 0:half], wa_s[0]) + dot(context[:, half:width], wa_s[1])
            first = x_s[rec, rows, :].astype(F32) + term
            first_s[rec, rows, :] = first
            position = start - CONV + at + lax.broadcasted_iota(jnp.int32, (size, 1), 0)
            valid = (position >= 0) & (position < lengths[rec])
            normed = norm_rows(first, 0.5 * gain_conv[...])
            held["input"] = jnp.where(valid, normed, 0.0).astype(BF16)

        def gate(part):
            glu = gated(dot(held["input"], wc_s[part, 0]), dot(held["input"], wc_s[part, 1]))
            glu = glu.astype(BF16).astype(F32)
            for tile in range(half // 128):
                glu_s[rec, part * (half // 128) + tile, rows, :] = glu[
                    :, tile * 128 : tile * 128 + 128
                ]

        return [project] + [functools.partial(gate, part) for part in range(2)]

    chunk = g_s.shape[1] - 24
    strip = 64
    conv_tiles = width // 128
    group_taps = 16

    def convolve(rec, at, tile):
        source = glu_s.at[rec, tile, pl.ds(at, chunk + CONV)]
        for shift in range(8):
            size = chunk + (CK - 1 - shift) // 8 * 8
            g_s[shift, pl.ds(0, size), :] = source[pl.ds(CONV - CK + 1 + shift, size), :].astype(
                BF16
            )
        taps = 0.5 * wd_s[tile]
        for top in range(0, chunk, strip):
            total = None
            for first_tap in range(0, CK, group_taps):
                group = None
                for tap in range(first_tap, min(first_tap + group_taps, CK)):
                    rows = pl.ds(top + tap // 8 * 8, strip)
                    product = taps[tap : tap + 1] * g_s[tap % 8, rows, :]
                    group = product if group is None else group + product
                group = group.astype(F32)
                total = group if total is None else total + group
            act_s[tile, pl.ds(at + top, strip), :] = gated(total, total).astype(BF16)

    tiles_all = wi_s.shape[0]
    out_copies = [
        pltpu.make_async_copy(out_s.at[rec], out.at[rec], o_sems.at[rec])
        for rec in range(rec_count)
    ]

    def enter(rec):
        for at in range(0, own, chunk):
            rows = pl.ds(at, chunk)
            sides = [
                jnp.concatenate([act_s[2 * side, rows, :], act_s[2 * side + 1, rows, :]], axis=1)
                for side in range(2)
            ]
            term = dot(sides[0], wo_s[0]) + dot(sides[1], wo_s[1])
            second = first_s[rec, pl.ds(at + CONV, chunk), :] + term
            second_s[rows, :] = second
            fin_s[rows, :] = norm_rows(second, 0.5 * gain_ffn[...]).astype(BF16)

    def up():
        @pl.loop(0, tiles_all // 2)
        def _(index):
            for at in range(2):
                hidden = dot(fin_s[...], wi_s[2 * index + at])
                hid_s[2 * index + at] = gated(hidden, hidden).astype(BF16)

    def down(rec, part):
        cols = pl.ds(part * 256, 256)
        total = second_s[:, cols]
        for tile in range(tiles_all):
            total = total + dot_nt(hid_s[tile], wf_s[tile, cols, :])
        position = start + lax.broadcasted_iota(jnp.int32, (own, 1), 0)
        out_s[rec, :, cols] = jnp.where(position < lengths[rec], total, 0.0).astype(BF16)

    def gate(rec, at):
        for piece in gated_frames(rec, at + CONV, chunk):
            piece()

    before = gated_frames(0, 0, CONV)
    before[0]()
    for copy in copies[2:4]:
        copy.wait()
    for load in ctx_copies[1:]:
        load.start()
    for load in loads[1:]:
        load[0]()
    for copy in copies[4:]:
        copy.start()
    for piece in before[1:]:
        piece()
    for at in range(0, own, chunk):
        gate(0, at)
    for copy in conv_copies:
        copy.wait()
    for rec in range(rec_count):
        if rec == 0:
            for at in range(0, own, chunk):

                @pl.loop(0, 2)
                def _(index):
                    for tile in range(conv_tiles // 2):
                        convolve(rec, at, index * (conv_tiles // 2) + tile)

        if rec + 1 < rec_count:
            ctx_copies[rec + 1].wait()
            loads[rec + 1][1]()
            for piece in gated_frames(rec + 1, 0, CONV):
                piece()
            for at in range(0, own, chunk):
                gate(rec + 1, at)
        if rec == 0:
            for copy in mid_copies:
                copy.wait()
        enter(rec)
        if rec == 0:
            for copy in late_copies:
                copy.wait()
        up()
        for part in range(width // 256):
            down(rec, part)
            if rec + 1 < rec_count:
                each = conv_tiles // (width // 256)
                for at in range(0, own, chunk):
                    for tile in range(each):
                        convolve(rec + 1, at, part * each + tile)
        out_copies[rec].start()
    for copy in out_copies:
        copy.wait()


def vmem(count):
    return [pl.BlockSpec(memory_space=pltpu.VMEM)] * count


def on_device(
    frames,
    lengths,
    memory_in,
    gain_attn,
    w_query,
    w_key,
    w_value,
    w_out,
    gain_conv,
    w_conv_in,
    w_depth,
    w_conv_out,
    gain_ffn,
    w_ffn_in,
    w_ffn_out,
):
    rec_count, frame_count, width = frames.shape
    blocks = lax.axis_size("tm")
    core_count = lax.axis_size("mp")
    core = lax.axis_index("mp")
    own = frame_count // core_count
    seg_block = frame_count // SEG

    def swapped(value):
        return lax.ppermute(value, "mp", [(0, 1), (1, 0)])

    memory = [memory_in]
    for reach in range(1, blocks):
        memory.append(lax.ppermute(memory_in, "tm", [(at, at ^ reach) for at in range(blocks)]))

    ring = [(2 * at, 2 * at + 2) for at in range(blocks - 1)] + [(2 * blocks - 2, 2 * blocks - 1)]
    ring += [(2 * at + 1, 2 * at - 1) for at in range(1, blocks)] + [(1, 0)]
    edge = lax.dynamic_slice_in_dim(frames, (1 - core) * (frame_count - HALO), HALO, 1)
    halo = lax.ppermute(edge, ("tm", "mp"), ring)

    wq, wk, wv = swapped(w_query), swapped(w_key), swapped(w_value)
    wo, wc = swapped(w_out), swapped(w_conv_in)
    wd, wco = swapped(w_depth), swapped(w_conv_out)
    wi, wf = swapped(w_ffn_in), swapped(w_ffn_out)

    ext = HALO + own + LOOK
    bank = seg_block * blocks
    keys = -(-(WINDOW + bank) // 128) * 128
    pairs = own // (2 * SEG)
    group = 2 * SEG + 8
    half = width // 2
    smem = pl.BlockSpec(memory_space=pltpu.SMEM)
    hbm = pl.BlockSpec(memory_space=pltpu.HBM)
    chunk = min(256, own)
    chunks = rec_count * (own // chunk)
    rows = rec_count * own
    hidden_half = w_ffn_in.shape[1]
    ctx, vectors = pl.pallas_call(
        functools.partial(attention_kernel, seg_block=seg_block, blocks=blocks),
        out_shape=(
            jax.ShapeDtypeStruct((rec_count, own + CONV, width), BF16),
            jax.ShapeDtypeStruct((rec_count, 4 * pairs, width), BF16),
        ),
        in_specs=[smem] + [hbm] * (10 + blocks) + vmem(1),
        out_specs=(hbm, vmem(1)[0]),
        scratch_shapes=[
            pltpu.VMEM((rec_count, ext, width), BF16),
            pltpu.VMEM((rec_count, ext, width), BF16),
            pltpu.VMEM((rec_count, ext, width), BF16),
            pltpu.VMEM((rec_count, ext, width), BF16),
            pltpu.VMEM((rec_count, ext, width), BF16),
            pltpu.VMEM((rec_count, bank, width), BF16),
            pltpu.VMEM((rec_count, bank, width), BF16),
            pltpu.VMEM((rec_count, bank, width), BF16),
            pltpu.VMEM((rec_count * pairs * 16, width), BF16),
            pltpu.VMEM((rec_count, own + CONV, width), BF16),
            pltpu.VMEM((rec_count, pairs * 8, width), F32),
            pltpu.VMEM((2, group, keys), F32),
            pltpu.VMEM((2, keys, width), BF16),
            pltpu.VMEM((2, width // 128, keys, 256), BF16),
            pltpu.VMEM((6, width, half), BF16),
            pltpu.VMEM((2, half, width), BF16),
            pltpu.SemaphoreType.DMA((rec_count, 3)),
            pltpu.SemaphoreType.DMA((blocks,)),
            pltpu.SemaphoreType.DMA((8,)),
            pltpu.SemaphoreType.DMA((rec_count,)),
        ],
        compiler_params=pltpu.CompilerParams(vmem_limit_bytes=67043328),
        cost_estimate=pl.CostEstimate(
            flops=10 * 2 * rows * width * half,
            bytes_accessed=8 << 20,
            transcendentals=rows * 2048,
        ),
        name="attend",
    )(
        lengths,
        frames,
        halo,
        *memory,
        w_query,
        wq,
        w_key,
        wk,
        w_value,
        wv,
        w_out,
        wo,
        gain_attn.reshape(1, width),
    )
    others = swapped(vectors)
    output = pl.pallas_call(
        convolution_kernel,
        out_shape=jax.ShapeDtypeStruct((rec_count, own, width), BF16),
        in_specs=[smem] + [hbm] * 15 + vmem(2),
        out_specs=hbm,
        scratch_shapes=[
            pltpu.VMEM((rec_count, own + CONV, width), BF16),
            pltpu.VMEM((rec_count, own + CONV, width), BF16),
            pltpu.VMEM((rec_count, own + CONV, width), F32),
            pltpu.VMEM((rec_count, width // 128, own + CONV, 128), F32),
            pltpu.VMEM((8, chunk + 24, 128), BF16),
            pltpu.VMEM((width // 128, own, 128), BF16),
            pltpu.VMEM((own, width), BF16),
            pltpu.VMEM((own, width), F32),
            pltpu.VMEM((hidden_half // 128, own, 256), BF16),
            pltpu.VMEM((rec_count, own, width), BF16),
            pltpu.VMEM((2, half, width), BF16),
            pltpu.VMEM((2, 2, width, half), BF16),
            pltpu.VMEM((width // 128, CK, 128), BF16),
            pltpu.VMEM((2, half, width), BF16),
            pltpu.VMEM((hidden_half // 128, width, 256), BF16),
            pltpu.VMEM((hidden_half // 128, width, 256), BF16),
            pltpu.SemaphoreType.DMA((rec_count, 4)),
            pltpu.SemaphoreType.DMA((6 + width // 128 + hidden_half // 64,)),
            pltpu.SemaphoreType.DMA((chunks,)),
        ],
        compiler_params=pltpu.CompilerParams(vmem_limit_bytes=65200 << 10),
        cost_estimate=pl.CostEstimate(
            flops=22 * 2 * rows * width * half,
            bytes_accessed=16 << 20,
            transcendentals=rows * 2560,
        ),
        name="rest",
    )(
        lengths,
        frames,
        halo,
        ctx,
        w_out,
        wo,
        w_conv_in,
        wc,
        w_depth,
        wd,
        w_conv_out,
        wco,
        w_ffn_in,
        wi,
        w_ffn_out,
        wf,
        gain_conv.reshape(1, width),
        gain_ffn.reshape(1, width),
    )
    memory_out = vectors + others
    return (output, memory_out)


def solution(mesh):
    placed = (
        P(("groups", "rec"), "tm", None),
        P(("groups", "rec")),
        P(("groups", "rec"), "tm", None),
        P(),
        P(None, "mp"),
        P(None, "mp"),
        P(None, "mp"),
        P("mp", None),
        P(),
        P(None, None, "mp"),
        P(None, "mp"),
        P("mp", None),
        P(),
        P(None, "mp"),
        P(None, "mp"),
    )
    return jax.shard_map(
        on_device,
        mesh=mesh,
        in_specs=placed,
        out_specs=(P(("groups", "rec"), ("tm", "mp"), None), P(("groups", "rec"), "tm", None)),
        check_vma=False,
    )
```

```python
import functools

import jax
import jax.numpy as jnp
from jax import lax
from jax.experimental import pallas as pl
from jax.experimental.pallas import tpu as pltpu
from jax.sharding import PartitionSpec as P


CK = 31
SEG = 64
LEFT = 32
LOOK = 16
DH = 64
EPSILON = 1e-05
NEGATIVE_FILL = -1e30

HALO = LEFT + SEG
CONV = 32
WINDOW = 2 * SEG + LEFT + LOOK

BF16 = jnp.bfloat16
F32 = jnp.float32


def norm_rows(rows, gain):
    average = jnp.mean(rows, axis=-1, keepdims=True)
    centred = rows - average
    spread = jnp.mean(centred * centred, axis=-1, keepdims=True)
    return centred * lax.rsqrt(spread + EPSILON) * gain


def dot(a, b):
    return jnp.dot(a, b, preferred_element_type=F32)


def dot_nt(a, b):
    return lax.dot_general(a, b, (((1,), (1,)), ((), ())), preferred_element_type=F32)


def gated(half_value, half_gate):
    return half_value + half_value * jnp.tanh(half_gate)


def load_around(rec, frames, halo, target, core, own, before, after, sems):
    def edges(side):
        if side == 0:
            pieces = [(halo, HALO - before, 0, before), (frames, own, before + own, after)]
        else:
            pieces = [(frames, own - before, 0, before), (halo, 0, before + own, after)]
        return [
            pltpu.make_async_copy(
                source.at[rec, pl.ds(at, size)], target.at[rec, pl.ds(to, size)], sems.at[1 + place]
            )
            for place, (source, at, to, size) in enumerate(pieces)
            if size
        ]

    body = pltpu.make_async_copy(
        frames.at[rec, pl.ds(pl.multiple_of(core * own, own), own)],
        target.at[rec, pl.ds(before, own)],
        sems.at[0],
    )

    def start():
        body.start()
        for side in range(2):

            @pl.when(core == side)
            def _():
                for copy in edges(side):
                    copy.start()

    def wait():
        body.wait()
        for side in range(2):

            @pl.when(core == side)
            def _():
                for copy in edges(side):
                    copy.wait()

    return start, wait


def copy_kernel(source, target):
    target[...] = source[...]


def attention_kernel(*refs, seg_block, blocks):
    lengths, frames, halo = refs[0:3]
    memory = refs[3 : 3 + blocks]
    weights = refs[3 + blocks : 11 + blocks]
    gain_attn = refs[11 + blocks]
    ctx_out, memory_out = refs[12 + blocks : 14 + blocks]
    (
        x_s,
        n_s,
        q_s,
        k_s,
        v_s,
        m_s,
        kb_s,
        vb_s,
        sq_s,
        ctx_s,
        sctx_s,
        bias_s,
        kcat_s,
        vcat_s,
        w_s,
        wa_s,
        sems,
        m_sems,
        w_sems,
        o_sems,
    ) = refs[14 + blocks :]
    rec_count, ext, width = x_s.shape
    own = ext - HALO - LOOK
    frame_count = frames.shape[1]
    bank = seg_block * blocks
    keys = kcat_s.shape[1]
    half = width // 2
    block = lax.axis_index("tm")
    core = lax.axis_index("mp")
    start = block * frame_count + core * own
    pairs = own // (2 * SEG)
    group_rows = 2 * SEG

    loads = [
        load_around(rec, frames, halo, x_s, core, own, HALO, LOOK, sems.at[rec])
        for rec in range(rec_count)
    ]
    loads[0][0]()
    memory_copies = [
        pltpu.make_async_copy(
            memory[at], m_s.at[:, pl.ds(at * seg_block, seg_block)], m_sems.at[at]
        )
        for at in range(blocks)
    ]
    targets = [w_s.at[at] for at in range(6)] + [wa_s.at[0], wa_s.at[1]]
    copies = [
        pltpu.make_async_copy(source, target, w_sems.at[at])
        for at, (source, target) in enumerate(zip(weights, targets))
    ]
    weight_copies, out_copies = copies[0:6], copies[6:8]
    for copy in weight_copies:
        copy.start()
    for load in loads[1:]:
        load[0]()
    for copy in memory_copies + out_copies:
        copy.start()
    kcat_s[...] = jnp.zeros_like(kcat_s)
    vcat_s[:, :, :, 0:128] = jnp.zeros(vcat_s.shape[0:3] + (128,), BF16)
    vcat_s[:, :, :, 128:256] = jnp.ones(vcat_s.shape[0:3] + (128,), BF16)
    wq_o, wq_p, wk_o, wk_p, wv_o, wv_p = [w_s.at[at] for at in range(6)]
    chunks = 3
    step = ext // chunks

    def normalise(rec, part):
        rows = pl.ds(part * step, step)
        normed = norm_rows(x_s[rec, rows, :].astype(F32), gain_attn[...]).astype(BF16)
        n_s[rec, rows, :] = normed
        return normed

    def project(rec, part, normed):
        rows = pl.ds(part * step, step)
        for side, (wq, wk, wv) in enumerate(((wq_o, wk_o, wv_o), (wq_p, wk_p, wv_p))):
            cols = pl.ds(side * half, half)
            q_s[rec, rows, cols] = (dot(normed, wq[...]) * DH**-0.5).astype(BF16)
            k_s[rec, rows, cols] = dot(normed, wk[...]).astype(BF16)
            v_s[rec, rows, cols] = dot(normed, wv[...]).astype(BF16)

    loads[0][1]()
    for part in range(chunks):
        normalise(0, part)
    for load in loads[1:]:
        load[1]()
    for copy in weight_copies:
        copy.wait()
    for rec in range(rec_count):
        for part in range(chunks):
            normed = n_s[rec, part * step : (part + 1) * step, :] if rec == 0 else normalise(rec, part)
            project(rec, part, normed)

    mean_rows = pairs * 16
    row_id = lax.broadcasted_iota(jnp.int32, (mean_rows, own), 0)
    col_id = lax.broadcasted_iota(jnp.int32, (mean_rows, own), 1)
    seg_of_row = jnp.where((row_id & 15) < 2, (row_id >> 4) * 2 + (row_id & 15), -1)
    averaging = jnp.where(seg_of_row == (col_id >> 6), 1.0 / SEG, 0.0).astype(BF16)
    summary = jnp.concatenate(
        [dot(averaging, n_s[rec, HALO : HALO + own, :]).astype(BF16) for rec in range(rec_count)],
        axis=0,
    )
    for copy in memory_copies:
        copy.wait()
    bank_rows = m_s[...].reshape(rec_count * bank, width)
    for part, (wq, wk, wv) in enumerate(((wq_o, wk_o, wv_o), (wq_p, wk_p, wv_p))):
        cols = pl.ds(part * half, half)
        kb_s[:, :, cols] = dot(bank_rows, wk[...]).astype(BF16).reshape(rec_count, bank, half)
        vb_s[:, :, cols] = dot(bank_rows, wv[...]).astype(BF16).reshape(rec_count, bank, half)
        sq_s[:, cols] = (dot(summary, wq[...]) * DH**-0.5).astype(BF16)

    lane = lax.broadcasted_iota(jnp.int32, (1, 128), 1)
    left_head = lane < DH

    def attend(place, rec, base, row_count, rows_padded, seg_first, load_queries, store):
        r_id = lax.broadcasted_iota(jnp.int32, (row_count, keys), 0)
        l_id = lax.broadcasted_iota(jnp.int32, (row_count, keys), 1)
        local = jnp.where(r_id < group_rows, r_id >> 6, r_id & 1)
        length = lengths[rec]
        position = start - HALO + base + l_id
        low = local * SEG
        in_window = (
            (l_id >= low)
            & (l_id < low + LEFT + SEG + LOOK)
            & (position >= 0)
            & (position < length)
            & (l_id < WINDOW)
        )
        slot_at = l_id - WINDOW
        slot = slot_at ^ (block * seg_block)
        in_bank = (
            (slot_at >= 0)
            & (slot_at < bank)
            & (slot < seg_first + local)
            & (slot * SEG < length)
        )
        bias_s[place, 0:row_count, :] = jnp.where(in_window | in_bank, 0.0, NEGATIVE_FILL)

        def scores_of(pair):
            cols = pl.ds(pair * 128, 128)
            kcat_s[place, 0:WINDOW, cols] = k_s[rec, pl.ds(pl.multiple_of(base, 16), WINDOW), cols]
            kcat_s[place, WINDOW : WINDOW + bank, cols] = kb_s[rec, :, cols]
            vcat_s[place, pair, 0:WINDOW, 0:128] = v_s[
                rec, pl.ds(pl.multiple_of(base, 16), WINDOW), cols
            ]
            vcat_s[place, pair, WINDOW : WINDOW + bank, 0:128] = vb_s[rec, :, cols]
            query = load_queries(cols)
            zero = jnp.zeros_like(query)
            both = jnp.concatenate(
                [jnp.where(left_head, query, zero), jnp.where(left_head, zero, query)], axis=0
            )
            return dot_nt(both, kcat_s[place, :, cols])

        def probs_of(scores):
            probs = []
            for side in range(2):
                part = scores[side * rows_padded : side * rows_padded + row_count]
                part = part + bias_s[place, 0:row_count, :]
                part = jnp.exp(part - jnp.max(part, axis=1, keepdims=True))
                part = part.astype(BF16)
                if rows_padded > row_count:
                    part = jnp.concatenate(
                        [part, jnp.zeros((rows_padded - row_count, keys), BF16)], axis=0
                    )
                probs.append(part)
            return jnp.concatenate(probs, axis=0)

        def mix(pair, probs):
            mixed = dot(probs, vcat_s[place, pair])
            sides = [
                mixed[side * rows_padded : side * rows_padded + row_count] for side in range(2)
            ]
            value = jnp.where(
                left_head,
                sides[0][:, 0:128] / sides[0][:, 128:256],
                sides[1][:, 0:128] / sides[1][:, 128:256],
            )
            store(pl.ds(pair * 128, 128), value)

        pair_count = width // 128
        scores = scores_of(0)
        for pair in range(pair_count):
            following = scores_of(pair + 1) if pair + 1 < pair_count else None
            mix(pair, probs_of(scores))
            scores = following

    def pair_of_segments(place, rec, pair):
        base = HALO - LEFT + pair * group_rows

        def load_queries(cols):
            return jnp.concatenate(
                [
                    q_s[rec, pl.ds(pl.multiple_of(base + LEFT, 16), group_rows), cols],
                    sq_s[pl.ds(pl.multiple_of((rec * pairs + pair) * 16, 16), 16), cols],
                ],
                axis=0,
            )

        def store(cols, value):
            ctx_s[rec, pl.ds(pl.multiple_of(CONV + pair * group_rows, 16), group_rows), cols] = (
                value[0:group_rows].astype(BF16)
            )
            sctx_s[rec, pl.ds(pl.multiple_of(pair * 8, 8), 8), cols] = value[group_rows:]

        attend(
            place,
            rec,
            base,
            group_rows + 8,
            group_rows + 16,
            start // SEG + 2 * pair,
            load_queries,
            store,
        )

    def segment_before(place, rec):
        def load_queries(cols):
            return q_s[rec, HALO - CONV : HALO, cols]

        def store(cols, value):
            ctx_s[rec, 0:CONV, cols] = value.astype(BF16)

        attend(place, rec, 0, CONV, CONV, start // SEG - 1, load_queries, store)

    ctx_copies = [
        pltpu.make_async_copy(ctx_s.at[rec], ctx_out.at[rec], o_sems.at[rec])
        for rec in range(rec_count)
    ]
    for rec in range(rec_count):
        segment_before(rec % 2, rec)
    for rec in range(rec_count):

        @pl.loop(0, pairs // 2)
        def _(index):
            for place in range(2):
                pair_of_segments(place, rec, 2 * index + place)

        ctx_copies[rec].start()

    for copy in out_copies:
        copy.wait()
    summed = sctx_s[...].reshape(rec_count * pairs * 8, width).astype(BF16)
    vectors = dot(summed[:, 0:half], wa_s[0]) + dot(summed[:, half:width], wa_s[1])
    memory_out[...] = jnp.zeros_like(memory_out)
    segs = 2 * pairs
    for side in range(2):

        @pl.when(core == side)
        def _():
            for rec in range(rec_count):
                rows = [
                    jnp.where(
                        start + seg * SEG < lengths[rec],
                        vectors[rec * pairs * 8 + seg // 2 * 8 + seg % 2 :][0:1],
                        0.0,
                    )
                    for seg in range(segs)
                ]
                memory_out[rec, side * segs : (side + 1) * segs, :] = jnp.concatenate(
                    rows, axis=0
                ).astype(BF16)

    for copy in ctx_copies:
        copy.wait()


def convolution_kernel(
    lengths,
    frames,
    halo,
    ctx,
    wa_o,
    wa_p,
    wc_o,
    wc_p,
    wd_o,
    wd_p,
    wo_o,
    wo_p,
    wi_o,
    wi_p,
    wf_o,
    wf_p,
    gain_conv,
    gain_ffn,
    out,
    x_s,
    ctx_s,
    first_s,
    glu_s,
    g_s,
    act_s,
    fin_s,
    second_s,
    hid_s,
    out_s,
    wa_s,
    wc_s,
    wd_s,
    wo_s,
    wi_s,
    wf_s,
    sems,
    w_sems,
    o_sems,
):
    rec_count, ext, width = x_s.shape
    own = ext - CONV
    half = width // 2
    core = lax.axis_index("mp")
    start = lax.axis_index("tm") * frames.shape[1] + core * own

    loads = [
        load_around(rec, frames, halo, x_s, core, own, CONV, 0, sems.at[rec])
        for rec in range(rec_count)
    ]
    ctx_copies = [
        pltpu.make_async_copy(ctx.at[rec], ctx_s.at[rec], sems.at[rec, 3])
        for rec in range(rec_count)
    ]
    pairs_of = []
    for target, sides in ((wa_s, (wa_o, wa_p)), (wc_s, (wc_o, wc_p)), (wo_s, (wo_o, wo_p))):
        pairs_of += [(sides[0], target.at[0]), (sides[1], target.at[1])]
    for tile in range(width // 128):
        cols = pl.ds(tile * 128 % half, 128)
        pairs_of.append(((wd_o, wd_p)[tile * 128 // half].at[:, cols], wd_s.at[tile]))
    tiles = wi_s.shape[0] // 2
    for target, sides in ((wi_s, (wi_o, wi_p)), (wf_s, (wf_o, wf_p))):
        for side in range(2):
            for tile in range(tiles):
                pairs_of.append(
                    (sides[side].at[:, pl.ds(tile * 256, 256)], target.at[side * tiles + tile])
                )
    copies = [
        pltpu.make_async_copy(source, target, w_sems.at[at])
        for at, (source, target) in enumerate(pairs_of)
    ]
    ctx_copies[0].start()
    for copy in copies[0:2]:
        copy.start()
    loads[0][0]()
    for copy in copies[2:4]:
        copy.start()
    ctx_copies[0].wait()
    loads[0][1]()
    for copy in copies[0:2]:
        copy.wait()
    mid_copies, conv_copies = copies[4:6], copies[6 : 6 + width // 128]
    late_copies = copies[6 + width // 128 :]

    def gated_frames(rec, at, size):
        rows = pl.ds(at if isinstance(at, int) else pl.multiple_of(at, 16), size)
        held = {}

        def project():
            context = ctx_s[rec, rows, :]
            term = dot(context[:, 0:half], wa_s[0]) + dot(context[:, half:width], wa_s[1])
            first = x_s[rec, rows, :].astype(F32) + term
            first_s[rec, rows, :] = first
            position = start - CONV + at + lax.broadcasted_iota(jnp.int32, (size, 1), 0)
            valid = (position >= 0) & (position < lengths[rec])
            normed = norm_rows(first, 0.5 * gain_conv[...])
            held["input"] = jnp.where(valid, normed, 0.0).astype(BF16)

        def gate(part):
            glu = gated(dot(held["input"], wc_s[part, 0]), dot(held["input"], wc_s[part, 1]))
            glu = glu.astype(BF16).astype(F32)
            for tile in range(half // 128):
                glu_s[rec, part * (half // 128) + tile, rows, :] = glu[
                    :, tile * 128 : tile * 128 + 128
                ]

        return [project] + [functools.partial(gate, part) for part in range(2)]

    chunk = g_s.shape[1] - 24
    chunks = own // chunk
    strip = 64
    conv_tiles = width // 128
    group_taps = 16

    def convolve(rec, at, tile):
        at = at if isinstance(at, int) else pl.multiple_of(at, chunk)
        source = glu_s.at[rec, tile, pl.ds(at, chunk + CONV)]
        for shift in range(8):
            size = chunk + (CK - 1 - shift) // 8 * 8
            g_s[shift, pl.ds(0, size), :] = source[pl.ds(CONV - CK + 1 + shift, size), :].astype(
                BF16
            )
        taps = 0.5 * wd_s[tile]
        for top in range(0, chunk, strip):
            total = None
            for first_tap in range(0, CK, group_taps):
                group = None
                for tap in range(first_tap, min(first_tap + group_taps, CK)):
                    rows = pl.ds(top + tap // 8 * 8, strip)
                    product = taps[tap : tap + 1] * g_s[tap % 8, rows, :]
                    group = product if group is None else group + product
                group = group.astype(F32)
                total = group if total is None else total + group
            act_s[tile, pl.ds(at + top, strip), :] = gated(total, total).astype(BF16)

    tiles_all = wi_s.shape[0]
    out_copies = [
        pltpu.make_async_copy(out_s.at[rec], out.at[rec], o_sems.at[rec])
        for rec in range(rec_count)
    ]

    def enter(rec):
        for at in range(0, own, chunk):
            rows = pl.ds(at, chunk)
            sides = [
                jnp.concatenate([act_s[2 * side, rows, :], act_s[2 * side + 1, rows, :]], axis=1)
                for side in range(2)
            ]
            term = dot(sides[0], wo_s[0]) + dot(sides[1], wo_s[1])
            second = first_s[rec, pl.ds(at + CONV, chunk), :] + term
            second_s[rows, :] = second
            fin_s[rows, :] = norm_rows(second, 0.5 * gain_ffn[...]).astype(BF16)

    def up():
        @pl.loop(0, tiles_all // 4)
        def _(index):
            for at in range(4):
                hidden = dot(fin_s[...], wi_s[4 * index + at])
                hid_s[4 * index + at] = gated(hidden, hidden).astype(BF16)

    def down(rec, part):
        cols = pl.ds(part * 256, 256)
        total = second_s[:, cols]
        for tile in range(tiles_all):
            total = total + dot_nt(hid_s[tile], wf_s[tile, cols, :])
        position = start + lax.broadcasted_iota(jnp.int32, (own, 1), 0)
        out_s[rec, :, cols] = jnp.where(position < lengths[rec], total, 0.0).astype(BF16)

    def down_beside(rec, conv_rec):
        units = chunks * conv_tiles // 2
        size = own // units

        @pl.loop(0, units)
        def _(index):
            rows = pl.ds(pl.multiple_of(index * size, size), size)
            total = second_s[rows, :]
            for tile in range(tiles_all):
                total = total + dot_nt(hid_s[tile, rows, :], wf_s[tile])
            position = start + index * size + lax.broadcasted_iota(jnp.int32, (size, 1), 0)
            out_s[rec, rows, :] = jnp.where(position < lengths[rec], total, 0.0).astype(BF16)
            for at in range(2):
                unit = 2 * index + at
                convolve(conv_rec, unit // conv_tiles * chunk, unit % conv_tiles)

    def gate(rec, at):
        for piece in gated_frames(rec, at + CONV, chunk):
            piece()

    before = gated_frames(0, 0, CONV)
    before[0]()
    for copy in copies[2:4]:
        copy.wait()
    for load in ctx_copies[1:]:
        load.start()
    for load in loads[1:]:
        load[0]()
    for copy in copies[4:]:
        copy.start()
    for piece in before[1:]:
        piece()
    for at in range(0, own, chunk):
        gate(0, at)
    for copy in conv_copies:
        copy.wait()
    for rec in range(rec_count):
        if rec == 0:
            for at in range(0, own, chunk):

                @pl.loop(0, 2)
                def _(index):
                    for tile in range(conv_tiles // 2):
                        convolve(rec, at, index * (conv_tiles // 2) + tile)

        if rec + 1 < rec_count:
            ctx_copies[rec + 1].wait()
            loads[rec + 1][1]()
            for piece in gated_frames(rec + 1, 0, CONV):
                piece()
            for at in range(0, own, chunk):
                gate(rec + 1, at)
        if rec == 0:
            for copy in mid_copies:
                copy.wait()
        enter(rec)
        if rec == 0:
            for copy in late_copies:
                copy.wait()
        up()
        if rec + 1 < rec_count:
            down_beside(rec, rec + 1)
        else:
            for part in range(width // 256):
                down(rec, part)
        out_copies[rec].start()
    for copy in out_copies:
        copy.wait()


def vmem(count):
    return [pl.BlockSpec(memory_space=pltpu.VMEM)] * count


def on_device(
    frames,
    lengths,
    memory_in,
    gain_attn,
    w_query,
    w_key,
    w_value,
    w_out,
    gain_conv,
    w_conv_in,
    w_depth,
    w_conv_out,
    gain_ffn,
    w_ffn_in,
    w_ffn_out,
):
    rec_count, frame_count, width = frames.shape
    blocks = lax.axis_size("tm")
    core_count = lax.axis_size("mp")
    core = lax.axis_index("mp")
    own = frame_count // core_count
    seg_block = frame_count // SEG

    def swapped(value):
        return lax.ppermute(value, "mp", [(0, 1), (1, 0)])

    memory = [memory_in]
    for reach in range(1, blocks):
        memory.append(lax.ppermute(memory_in, "tm", [(at, at ^ reach) for at in range(blocks)]))

    ring = [(2 * at, 2 * at + 2) for at in range(blocks - 1)] + [(2 * blocks - 2, 2 * blocks - 1)]
    ring += [(2 * at + 1, 2 * at - 1) for at in range(1, blocks)] + [(1, 0)]
    edge = lax.dynamic_slice_in_dim(frames, (1 - core) * (frame_count - HALO), HALO, 1)
    halo = lax.ppermute(edge, ("tm", "mp"), ring)

    wq, wk, wv = swapped(w_query), swapped(w_key), swapped(w_value)
    wo, wc = swapped(w_out), swapped(w_conv_in)
    wd, wco = swapped(w_depth), swapped(w_conv_out)
    wi, wf = swapped(w_ffn_in), swapped(w_ffn_out)

    ext = HALO + own + LOOK
    bank = seg_block * blocks
    keys = -(-(WINDOW + bank) // 128) * 128
    pairs = own // (2 * SEG)
    group = 2 * SEG + 8
    half = width // 2
    smem = pl.BlockSpec(memory_space=pltpu.SMEM)
    hbm = pl.BlockSpec(memory_space=pltpu.HBM)
    chunk = min(256, own)
    chunks = rec_count * (own // chunk)
    rows = rec_count * own
    hidden_half = w_ffn_in.shape[1]
    gain_first = pl.pallas_call(
        copy_kernel,
        out_shape=jax.ShapeDtypeStruct((1, width), F32),
        in_specs=vmem(1),
        out_specs=vmem(1)[0],
        compiler_params=pltpu.CompilerParams(vmem_limit_bytes=67043328),
        name="hold",
    )(gain_attn.reshape(1, width))
    ctx, vectors = pl.pallas_call(
        functools.partial(attention_kernel, seg_block=seg_block, blocks=blocks),
        out_shape=(
            jax.ShapeDtypeStruct((rec_count, own + CONV, width), BF16),
            jax.ShapeDtypeStruct((rec_count, 4 * pairs, width), BF16),
        ),
        in_specs=[smem] + [hbm] * (10 + blocks) + vmem(1),
        out_specs=(hbm, vmem(1)[0]),
        scratch_shapes=[
            pltpu.VMEM((rec_count, ext, width), BF16),
            pltpu.VMEM((rec_count, ext, width), BF16),
            pltpu.VMEM((rec_count, ext, width), BF16),
            pltpu.VMEM((rec_count, ext, width), BF16),
            pltpu.VMEM((rec_count, ext, width), BF16),
            pltpu.VMEM((rec_count, bank, width), BF16),
            pltpu.VMEM((rec_count, bank, width), BF16),
            pltpu.VMEM((rec_count, bank, width), BF16),
            pltpu.VMEM((rec_count * pairs * 16, width), BF16),
            pltpu.VMEM((rec_count, own + CONV, width), BF16),
            pltpu.VMEM((rec_count, pairs * 8, width), F32),
            pltpu.VMEM((2, group, keys), F32),
            pltpu.VMEM((2, keys, width), BF16),
            pltpu.VMEM((2, width // 128, keys, 256), BF16),
            pltpu.VMEM((6, width, half), BF16),
            pltpu.VMEM((2, half, width), BF16),
            pltpu.SemaphoreType.DMA((rec_count, 3)),
            pltpu.SemaphoreType.DMA((blocks,)),
            pltpu.SemaphoreType.DMA((8,)),
            pltpu.SemaphoreType.DMA((rec_count,)),
        ],
        compiler_params=pltpu.CompilerParams(vmem_limit_bytes=67043328),
        cost_estimate=pl.CostEstimate(
            flops=10 * 2 * rows * width * half,
            bytes_accessed=8 << 20,
            transcendentals=rows * 2048,
        ),
        name="attend",
    )(lengths, frames, halo, *memory, w_query, wq, w_key, wk, w_value, wv, w_out, wo, gain_first)
    others = swapped(vectors)
    output = pl.pallas_call(
        convolution_kernel,
        out_shape=jax.ShapeDtypeStruct((rec_count, own, width), BF16),
        in_specs=[smem] + [hbm] * 15 + vmem(2),
        out_specs=hbm,
        scratch_shapes=[
            pltpu.VMEM((rec_count, own + CONV, width), BF16),
            pltpu.VMEM((rec_count, own + CONV, width), BF16),
            pltpu.VMEM((rec_count, own + CONV, width), F32),
            pltpu.VMEM((rec_count, width // 128, own + CONV, 128), F32),
            pltpu.VMEM((8, chunk + 24, 128), BF16),
            pltpu.VMEM((width // 128, own, 128), BF16),
            pltpu.VMEM((own, width), BF16),
            pltpu.VMEM((own, width), F32),
            pltpu.VMEM((hidden_half // 128, own, 256), BF16),
            pltpu.VMEM((rec_count, own, width), BF16),
            pltpu.VMEM((2, half, width), BF16),
            pltpu.VMEM((2, 2, width, half), BF16),
            pltpu.VMEM((width // 128, CK, 128), BF16),
            pltpu.VMEM((2, half, width), BF16),
            pltpu.VMEM((hidden_half // 128, width, 256), BF16),
            pltpu.VMEM((hidden_half // 128, width, 256), BF16),
            pltpu.SemaphoreType.DMA((rec_count, 4)),
            pltpu.SemaphoreType.DMA((6 + width // 128 + hidden_half // 64,)),
            pltpu.SemaphoreType.DMA((chunks,)),
        ],
        compiler_params=pltpu.CompilerParams(vmem_limit_bytes=65200 << 10),
        cost_estimate=pl.CostEstimate(
            flops=22 * 2 * rows * width * half,
            bytes_accessed=16 << 20,
            transcendentals=rows * 2560,
        ),
        name="rest",
    )(
        lengths,
        frames,
        halo,
        ctx,
        w_out,
        wo,
        w_conv_in,
        wc,
        w_depth,
        wd,
        w_conv_out,
        wco,
        w_ffn_in,
        wi,
        w_ffn_out,
        wf,
        gain_conv.reshape(1, width),
        gain_ffn.reshape(1, width),
    )
    memory_out = vectors + others
    return (output, memory_out)


def solution(mesh):
    placed = (
        P(("groups", "rec"), "tm", None),
        P(("groups", "rec")),
        P(("groups", "rec"), "tm", None),
        P(),
        P(None, "mp"),
        P(None, "mp"),
        P(None, "mp"),
        P("mp", None),
        P(),
        P(None, None, "mp"),
        P(None, "mp"),
        P("mp", None),
        P(),
        P(None, "mp"),
        P(None, "mp"),
    )
    return jax.shard_map(
        on_device,
        mesh=mesh,
        in_specs=placed,
        out_specs=(P(("groups", "rec"), ("tm", "mp"), None), P(("groups", "rec"), "tm", None)),
        check_vma=False,
    )
```

```python
import functools

import jax
import jax.numpy as jnp
from jax import lax
from jax.experimental import pallas as pl
from jax.experimental.pallas import tpu as pltpu
from jax.sharding import PartitionSpec as P


CK = 31
SEG = 64
LEFT = 32
LOOK = 16
DH = 64
EPSILON = 1e-05
NEGATIVE_FILL = -1e30

HALO = LEFT + SEG
CONV = 32
WINDOW = 2 * SEG + LEFT + LOOK

BF16 = jnp.bfloat16
F32 = jnp.float32


def norm_rows(rows, gain):
    average = jnp.mean(rows, axis=-1, keepdims=True)
    centred = rows - average
    spread = jnp.mean(centred * centred, axis=-1, keepdims=True)
    return centred * lax.rsqrt(spread + EPSILON) * gain


def dot(a, b):
    return jnp.dot(a, b, preferred_element_type=F32)


def dot_nt(a, b):
    return lax.dot_general(a, b, (((1,), (1,)), ((), ())), preferred_element_type=F32)


def gated(half_value, half_gate):
    return half_value + half_value * jnp.tanh(half_gate)


def load_around(rec, frames, halo, target, core, own, before, after, sems):
    def edges(side):
        if side == 0:
            pieces = [(halo, HALO - before, 0, before), (frames, own, before + own, after)]
        else:
            pieces = [(frames, own - before, 0, before), (halo, 0, before + own, after)]
        return [
            pltpu.make_async_copy(
                source.at[rec, pl.ds(at, size)], target.at[rec, pl.ds(to, size)], sems.at[1 + place]
            )
            for place, (source, at, to, size) in enumerate(pieces)
            if size
        ]

    body = pltpu.make_async_copy(
        frames.at[rec, pl.ds(pl.multiple_of(core * own, own), own)],
        target.at[rec, pl.ds(before, own)],
        sems.at[0],
    )

    def start():
        body.start()
        for side in range(2):

            @pl.when(core == side)
            def _():
                for copy in edges(side):
                    copy.start()

    def wait():
        body.wait()
        for side in range(2):

            @pl.when(core == side)
            def _():
                for copy in edges(side):
                    copy.wait()

    return start, wait


def copy_kernel(source, target):
    target[...] = source[...]


def attention_kernel(*refs, seg_block, blocks):
    lengths, frames, halo = refs[0:3]
    memory = refs[3 : 3 + blocks]
    weights = refs[3 + blocks : 11 + blocks]
    gain_attn = refs[11 + blocks]
    ctx_out, memory_out = refs[12 + blocks : 14 + blocks]
    (
        x_s,
        n_s,
        q_s,
        k_s,
        v_s,
        m_s,
        kb_s,
        vb_s,
        sq_s,
        ctx_s,
        sctx_s,
        bias_s,
        kcat_s,
        vcat_s,
        w_s,
        wa_s,
        sems,
        m_sems,
        w_sems,
        o_sems,
    ) = refs[14 + blocks :]
    rec_count, ext, width = x_s.shape
    own = ext - HALO - LOOK
    frame_count = frames.shape[1]
    bank = seg_block * blocks
    keys = kcat_s.shape[1]
    half = width // 2
    block = lax.axis_index("tm")
    core = lax.axis_index("mp")
    start = block * frame_count + core * own
    pairs = own // (2 * SEG)
    group_rows = 2 * SEG

    loads = [
        load_around(rec, frames, halo, x_s, core, own, HALO, LOOK, sems.at[rec])
        for rec in range(rec_count)
    ]
    loads[0][0]()
    memory_copies = [
        pltpu.make_async_copy(
            memory[at], m_s.at[:, pl.ds(at * seg_block, seg_block)], m_sems.at[at]
        )
        for at in range(blocks)
    ]
    targets = [w_s.at[at] for at in range(6)] + [wa_s.at[0], wa_s.at[1]]
    copies = [
        pltpu.make_async_copy(source, target, w_sems.at[at])
        for at, (source, target) in enumerate(zip(weights, targets))
    ]
    weight_copies, out_copies = copies[0:6], copies[6:8]
    for copy in weight_copies:
        copy.start()
    for load in loads[1:]:
        load[0]()
    for copy in memory_copies + out_copies:
        copy.start()
    kcat_s[...] = jnp.zeros_like(kcat_s)
    vcat_s[:, :, :, 0:128] = jnp.zeros(vcat_s.shape[0:3] + (128,), BF16)
    vcat_s[:, :, :, 128:256] = jnp.ones(vcat_s.shape[0:3] + (128,), BF16)
    wq_o, wq_p, wk_o, wk_p, wv_o, wv_p = [w_s.at[at] for at in range(6)]
    chunks = 3
    step = ext // chunks

    def normalise(rec, part):
        rows = pl.ds(part * step, step)
        normed = norm_rows(x_s[rec, rows, :].astype(F32), gain_attn[...]).astype(BF16)
        n_s[rec, rows, :] = normed
        return normed

    def project(rec, part, normed):
        rows = pl.ds(part * step, step)
        for side, (wq, wk, wv) in enumerate(((wq_o, wk_o, wv_o), (wq_p, wk_p, wv_p))):
            cols = pl.ds(side * half, half)
            q_s[rec, rows, cols] = (dot(normed, wq[...]) * DH**-0.5).astype(BF16)
            k_s[rec, rows, cols] = dot(normed, wk[...]).astype(BF16)
            v_s[rec, rows, cols] = dot(normed, wv[...]).astype(BF16)

    loads[0][1]()
    for part in range(chunks):
        normalise(0, part)
    for load in loads[1:]:
        load[1]()
    for copy in weight_copies:
        copy.wait()
    for rec in range(rec_count):
        for part in range(chunks):
            normed = n_s[rec, part * step : (part + 1) * step, :] if rec == 0 else normalise(rec, part)
            project(rec, part, normed)

    mean_rows = pairs * 16
    row_id = lax.broadcasted_iota(jnp.int32, (mean_rows, own), 0)
    col_id = lax.broadcasted_iota(jnp.int32, (mean_rows, own), 1)
    seg_of_row = jnp.where((row_id & 15) < 2, (row_id >> 4) * 2 + (row_id & 15), -1)
    averaging = jnp.where(seg_of_row == (col_id >> 6), 1.0 / SEG, 0.0).astype(BF16)
    summary = jnp.concatenate(
        [dot(averaging, n_s[rec, HALO : HALO + own, :]).astype(BF16) for rec in range(rec_count)],
        axis=0,
    )
    for copy in memory_copies:
        copy.wait()
    bank_rows = m_s[...].reshape(rec_count * bank, width)
    for part, (wq, wk, wv) in enumerate(((wq_o, wk_o, wv_o), (wq_p, wk_p, wv_p))):
        cols = pl.ds(part * half, half)
        kb_s[:, :, cols] = dot(bank_rows, wk[...]).astype(BF16).reshape(rec_count, bank, half)
        vb_s[:, :, cols] = dot(bank_rows, wv[...]).astype(BF16).reshape(rec_count, bank, half)
        sq_s[:, cols] = (dot(summary, wq[...]) * DH**-0.5).astype(BF16)

    lane = lax.broadcasted_iota(jnp.int32, (1, 128), 1)
    left_head = lane < DH

    def attend(place, rec, base, row_count, rows_padded, seg_first, load_queries, store):
        r_id = lax.broadcasted_iota(jnp.int32, (row_count, keys), 0)
        l_id = lax.broadcasted_iota(jnp.int32, (row_count, keys), 1)
        local = jnp.where(r_id < group_rows, r_id >> 6, r_id & 1)
        length = lengths[rec]
        position = start - HALO + base + l_id
        low = local * SEG
        in_window = (
            (l_id >= low)
            & (l_id < low + LEFT + SEG + LOOK)
            & (position >= 0)
            & (position < length)
            & (l_id < WINDOW)
        )
        slot_at = l_id - WINDOW
        slot = slot_at ^ (block * seg_block)
        in_bank = (
            (slot_at >= 0)
            & (slot_at < bank)
            & (slot < seg_first + local)
            & (slot * SEG < length)
        )
        bias_s[place, 0:row_count, :] = jnp.where(in_window | in_bank, 0.0, NEGATIVE_FILL)

        def scores_of(pair):
            cols = pl.ds(pair * 128, 128)
            kcat_s[place, 0:WINDOW, cols] = k_s[rec, pl.ds(pl.multiple_of(base, 16), WINDOW), cols]
            kcat_s[place, WINDOW : WINDOW + bank, cols] = kb_s[rec, :, cols]
            vcat_s[place, pair, 0:WINDOW, 0:128] = v_s[
                rec, pl.ds(pl.multiple_of(base, 16), WINDOW), cols
            ]
            vcat_s[place, pair, WINDOW : WINDOW + bank, 0:128] = vb_s[rec, :, cols]
            query = load_queries(cols)
            zero = jnp.zeros_like(query)
            both = jnp.concatenate(
                [jnp.where(left_head, query, zero), jnp.where(left_head, zero, query)], axis=0
            )
            return dot_nt(both, kcat_s[place, :, cols])

        def probs_of(scores):
            probs = []
            for side in range(2):
                part = scores[side * rows_padded : side * rows_padded + row_count]
                part = part + bias_s[place, 0:row_count, :]
                part = jnp.exp(part - jnp.max(part, axis=1, keepdims=True))
                part = part.astype(BF16)
                if rows_padded > row_count:
                    part = jnp.concatenate(
                        [part, jnp.zeros((rows_padded - row_count, keys), BF16)], axis=0
                    )
                probs.append(part)
            return jnp.concatenate(probs, axis=0)

        def mix(pair, probs):
            mixed = dot(probs, vcat_s[place, pair])
            sides = [
                mixed[side * rows_padded : side * rows_padded + row_count] for side in range(2)
            ]
            value = jnp.where(
                left_head,
                sides[0][:, 0:128] / sides[0][:, 128:256],
                sides[1][:, 0:128] / sides[1][:, 128:256],
            )
            store(pl.ds(pair * 128, 128), value)

        pair_count = width // 128
        scores = scores_of(0)
        for pair in range(pair_count):
            following = scores_of(pair + 1) if pair + 1 < pair_count else None
            mix(pair, probs_of(scores))
            scores = following

    def pair_of_segments(place, rec, pair):
        base = HALO - LEFT + pair * group_rows

        def load_queries(cols):
            return jnp.concatenate(
                [
                    q_s[rec, pl.ds(pl.multiple_of(base + LEFT, 16), group_rows), cols],
                    sq_s[pl.ds(pl.multiple_of((rec * pairs + pair) * 16, 16), 16), cols],
                ],
                axis=0,
            )

        def store(cols, value):
            ctx_s[rec, pl.ds(pl.multiple_of(CONV + pair * group_rows, 16), group_rows), cols] = (
                value[0:group_rows].astype(BF16)
            )
            sctx_s[rec, pl.ds(pl.multiple_of(pair * 8, 8), 8), cols] = value[group_rows:]

        attend(
            place,
            rec,
            base,
            group_rows + 8,
            group_rows + 16,
            start // SEG + 2 * pair,
            load_queries,
            store,
        )

    def segment_before(place, rec):
        def load_queries(cols):
            return q_s[rec, HALO - CONV : HALO, cols]

        def store(cols, value):
            ctx_s[rec, 0:CONV, cols] = value.astype(BF16)

        attend(place, rec, 0, CONV, CONV, start // SEG - 1, load_queries, store)

    ctx_copies = [
        pltpu.make_async_copy(ctx_s.at[rec], ctx_out.at[rec], o_sems.at[rec])
        for rec in range(rec_count)
    ]
    for rec in range(rec_count):
        segment_before(rec % 2, rec)
    for rec in range(rec_count):

        @pl.loop(0, pairs // 2)
        def _(index):
            for place in range(2):
                pair_of_segments(place, rec, 2 * index + place)

        ctx_copies[rec].start()

    for copy in out_copies:
        copy.wait()
    summed = sctx_s[...].reshape(rec_count * pairs * 8, width).astype(BF16)
    vectors = dot(summed[:, 0:half], wa_s[0]) + dot(summed[:, half:width], wa_s[1])
    memory_out[...] = jnp.zeros_like(memory_out)
    segs = 2 * pairs
    for side in range(2):

        @pl.when(core == side)
        def _():
            for rec in range(rec_count):
                rows = [
                    jnp.where(
                        start + seg * SEG < lengths[rec],
                        vectors[rec * pairs * 8 + seg // 2 * 8 + seg % 2 :][0:1],
                        0.0,
                    )
                    for seg in range(segs)
                ]
                memory_out[rec, side * segs : (side + 1) * segs, :] = jnp.concatenate(
                    rows, axis=0
                ).astype(BF16)

    for copy in ctx_copies:
        copy.wait()


def convolution_kernel(
    lengths,
    frames,
    halo,
    ctx,
    wa_o,
    wa_p,
    wc_o,
    wc_p,
    wd_o,
    wd_p,
    wo_o,
    wo_p,
    wi_o,
    wi_p,
    wf_o,
    wf_p,
    gain_conv,
    gain_ffn,
    out,
    x_s,
    ctx_s,
    first_s,
    glu_s,
    g_s,
    act_s,
    fin_s,
    second_s,
    hid_s,
    out_s,
    wa_s,
    wc_s,
    wd_s,
    wo_s,
    wi_s,
    wf_s,
    sems,
    w_sems,
    o_sems,
):
    rec_count, ext, width = x_s.shape
    own = ext - CONV
    half = width // 2
    core = lax.axis_index("mp")
    start = lax.axis_index("tm") * frames.shape[1] + core * own

    loads = [
        load_around(rec, frames, halo, x_s, core, own, CONV, 0, sems.at[rec])
        for rec in range(rec_count)
    ]
    ctx_copies = [
        pltpu.make_async_copy(ctx.at[rec], ctx_s.at[rec], sems.at[rec, 3])
        for rec in range(rec_count)
    ]
    pairs_of = []
    for target, sides in ((wa_s, (wa_o, wa_p)), (wc_s, (wc_o, wc_p)), (wo_s, (wo_o, wo_p))):
        pairs_of += [(sides[0], target.at[0]), (sides[1], target.at[1])]
    for tile in range(width // 128):
        cols = pl.ds(tile * 128 % half, 128)
        pairs_of.append(((wd_o, wd_p)[tile * 128 // half].at[:, cols], wd_s.at[tile]))
    tiles = wi_s.shape[0] // 2
    for target, sides in ((wi_s, (wi_o, wi_p)), (wf_s, (wf_o, wf_p))):
        for side in range(2):
            for tile in range(tiles):
                pairs_of.append(
                    (sides[side].at[:, pl.ds(tile * 256, 256)], target.at[side * tiles + tile])
                )
    copies = [
        pltpu.make_async_copy(source, target, w_sems.at[at])
        for at, (source, target) in enumerate(pairs_of)
    ]
    ctx_copies[0].start()
    for copy in copies[0:2]:
        copy.start()
    loads[0][0]()
    for copy in copies[2:4]:
        copy.start()
    ctx_copies[0].wait()
    loads[0][1]()
    for copy in copies[0:2]:
        copy.wait()
    mid_copies, conv_copies = copies[4:6], copies[6 : 6 + width // 128]
    late_copies = copies[6 + width // 128 :]

    def gated_frames(rec, at, size):
        rows = pl.ds(at if isinstance(at, int) else pl.multiple_of(at, 16), size)
        held = {}

        def project():
            context = ctx_s[rec, rows, :]
            term = dot(context[:, 0:half], wa_s[0]) + dot(context[:, half:width], wa_s[1])
            first = x_s[rec, rows, :].astype(F32) + term
            first_s[rec, rows, :] = first
            position = start - CONV + at + lax.broadcasted_iota(jnp.int32, (size, 1), 0)
            valid = (position >= 0) & (position < lengths[rec])
            normed = norm_rows(first, 0.5 * gain_conv[...])
            held["input"] = jnp.where(valid, normed, 0.0).astype(BF16)

        def gate(part):
            glu = gated(dot(held["input"], wc_s[part, 0]), dot(held["input"], wc_s[part, 1]))
            glu = glu.astype(BF16).astype(F32)
            for tile in range(half // 128):
                glu_s[rec, part * (half // 128) + tile, rows, :] = glu[
                    :, tile * 128 : tile * 128 + 128
                ]

        return [project] + [functools.partial(gate, part) for part in range(2)]

    chunk = g_s.shape[1] - 24
    chunks = own // chunk
    strip = 32
    conv_tiles = width // 128
    group_taps = 16

    def convolve(rec, at, tile):
        at = at if isinstance(at, int) else pl.multiple_of(at, chunk)
        source = glu_s.at[rec, tile, pl.ds(at, chunk + CONV)]
        for shift in range(8):
            size = chunk + (CK - 1 - shift) // 8 * 8
            g_s[shift, pl.ds(0, size), :] = source[pl.ds(CONV - CK + 1 + shift, size), :].astype(
                BF16
            )
        taps = 0.5 * wd_s[tile]
        for top in range(0, chunk, strip):
            total = None
            for first_tap in range(0, CK, group_taps):
                group = None
                for tap in range(first_tap, min(first_tap + group_taps, CK)):
                    rows = pl.ds(top + tap // 8 * 8, strip)
                    product = taps[tap : tap + 1] * g_s[tap % 8, rows, :]
                    group = product if group is None else group + product
                group = group.astype(F32)
                total = group if total is None else total + group
            act_s[tile, pl.ds(at + top, strip), :] = gated(total, total).astype(BF16)

    tiles_all = wi_s.shape[0]
    out_copies = [
        pltpu.make_async_copy(out_s.at[rec], out.at[rec], o_sems.at[rec])
        for rec in range(rec_count)
    ]
    out_halves = [
        pltpu.make_async_copy(
            out_s.at[rec_count - 1, :, pl.ds(part * 256, 256)],
            out.at[rec_count - 1, :, pl.ds(part * 256, 256)],
            o_sems.at[rec_count - 1 + part],
        )
        for part in range(width // 256)
    ]

    def enter(rec):
        for at in range(0, own, chunk):
            rows = pl.ds(at, chunk)
            sides = [
                jnp.concatenate([act_s[2 * side, rows, :], act_s[2 * side + 1, rows, :]], axis=1)
                for side in range(2)
            ]
            term = dot(sides[0], wo_s[0]) + dot(sides[1], wo_s[1])
            second = first_s[rec, pl.ds(at + CONV, chunk), :] + term
            second_s[rows, :] = second
            fin_s[rows, :] = norm_rows(second, 0.5 * gain_ffn[...]).astype(BF16)

    def up():
        @pl.loop(0, tiles_all // 4)
        def _(index):
            for at in range(4):
                hidden = dot(fin_s[...], wi_s[4 * index + at])
                hid_s[4 * index + at] = gated(hidden, hidden).astype(BF16)

    def down(rec, part):
        cols = pl.ds(part * 256, 256)
        total = second_s[:, cols]
        for tile in range(tiles_all):
            total = total + dot_nt(hid_s[tile], wf_s[tile, cols, :])
        position = start + lax.broadcasted_iota(jnp.int32, (own, 1), 0)
        out_s[rec, :, cols] = jnp.where(position < lengths[rec], total, 0.0).astype(BF16)

    def down_beside(rec, conv_rec):
        units = chunks * conv_tiles // 2
        size = own // units

        @pl.loop(0, units)
        def _(index):
            rows = pl.ds(pl.multiple_of(index * size, size), size)
            total = second_s[rows, :]
            for tile in range(tiles_all):
                total = total + dot_nt(hid_s[tile, rows, :], wf_s[tile])
            position = start + index * size + lax.broadcasted_iota(jnp.int32, (size, 1), 0)
            out_s[rec, rows, :] = jnp.where(position < lengths[rec], total, 0.0).astype(BF16)
            for at in range(2):
                unit = 2 * index + at
                convolve(conv_rec, unit // conv_tiles * chunk, unit % conv_tiles)

    def gate(rec, at):
        for piece in gated_frames(rec, at + CONV, chunk):
            piece()

    before = gated_frames(0, 0, CONV)
    before[0]()
    for copy in copies[2:4]:
        copy.wait()
    for load in ctx_copies[1:]:
        load.start()
    for load in loads[1:]:
        load[0]()
    for copy in copies[4:]:
        copy.start()
    for piece in before[1:]:
        piece()
    for at in range(0, own, chunk):
        gate(0, at)
    for copy in conv_copies:
        copy.wait()
    for rec in range(rec_count):
        if rec == 0:
            for at in range(0, own, chunk):

                @pl.loop(0, 2)
                def _(index):
                    for tile in range(conv_tiles // 2):
                        convolve(rec, at, index * (conv_tiles // 2) + tile)

        if rec + 1 < rec_count:
            ctx_copies[rec + 1].wait()
            loads[rec + 1][1]()
            for piece in gated_frames(rec + 1, 0, CONV):
                piece()
            for at in range(0, own, chunk):
                gate(rec + 1, at)
        if rec == 0:
            for copy in mid_copies:
                copy.wait()
        enter(rec)
        if rec == 0:
            for copy in late_copies[: len(late_copies) // 2]:
                copy.wait()
        up()
        if rec == 0:
            for copy in late_copies[len(late_copies) // 2 :]:
                copy.wait()
        if rec + 1 < rec_count:
            down_beside(rec, rec + 1)
        else:
            for part in range(width // 256):
                down(rec, part)
                out_halves[part].start()
        if rec + 1 < rec_count:
            out_copies[rec].start()
    for copy in out_copies[:-1] + out_halves:
        copy.wait()


def vmem(count):
    return [pl.BlockSpec(memory_space=pltpu.VMEM)] * count


def on_device(
    frames,
    lengths,
    memory_in,
    gain_attn,
    w_query,
    w_key,
    w_value,
    w_out,
    gain_conv,
    w_conv_in,
    w_depth,
    w_conv_out,
    gain_ffn,
    w_ffn_in,
    w_ffn_out,
):
    rec_count, frame_count, width = frames.shape
    blocks = lax.axis_size("tm")
    core_count = lax.axis_size("mp")
    core = lax.axis_index("mp")
    own = frame_count // core_count
    seg_block = frame_count // SEG

    def swapped(value):
        return lax.ppermute(value, "mp", [(0, 1), (1, 0)])

    memory = [memory_in]
    for reach in range(1, blocks):
        memory.append(lax.ppermute(memory_in, "tm", [(at, at ^ reach) for at in range(blocks)]))

    ring = [(2 * at, 2 * at + 2) for at in range(blocks - 1)] + [(2 * blocks - 2, 2 * blocks - 1)]
    ring += [(2 * at + 1, 2 * at - 1) for at in range(1, blocks)] + [(1, 0)]
    edge = lax.dynamic_slice_in_dim(frames, (1 - core) * (frame_count - HALO), HALO, 1)
    halo = lax.ppermute(edge, ("tm", "mp"), ring)

    wq, wk, wv = swapped(w_query), swapped(w_key), swapped(w_value)
    wo, wc = swapped(w_out), swapped(w_conv_in)
    wd, wco = swapped(w_depth), swapped(w_conv_out)
    wi, wf = swapped(w_ffn_in), swapped(w_ffn_out)

    ext = HALO + own + LOOK
    bank = seg_block * blocks
    keys = -(-(WINDOW + bank) // 128) * 128
    pairs = own // (2 * SEG)
    group = 2 * SEG + 8
    half = width // 2
    smem = pl.BlockSpec(memory_space=pltpu.SMEM)
    hbm = pl.BlockSpec(memory_space=pltpu.HBM)
    chunk = min(256, own)
    chunks = rec_count * (own // chunk)
    rows = rec_count * own
    hidden_half = w_ffn_in.shape[1]
    gain_first = pl.pallas_call(
        copy_kernel,
        out_shape=jax.ShapeDtypeStruct((1, width), F32),
        in_specs=vmem(1),
        out_specs=vmem(1)[0],
        compiler_params=pltpu.CompilerParams(vmem_limit_bytes=67043328),
        name="hold",
    )(gain_attn.reshape(1, width))
    ctx, vectors = pl.pallas_call(
        functools.partial(attention_kernel, seg_block=seg_block, blocks=blocks),
        out_shape=(
            jax.ShapeDtypeStruct((rec_count, own + CONV, width), BF16),
            jax.ShapeDtypeStruct((rec_count, 4 * pairs, width), BF16),
        ),
        in_specs=[smem] + [hbm] * (10 + blocks) + vmem(1),
        out_specs=(hbm, vmem(1)[0]),
        scratch_shapes=[
            pltpu.VMEM((rec_count, ext, width), BF16),
            pltpu.VMEM((rec_count, ext, width), BF16),
            pltpu.VMEM((rec_count, ext, width), BF16),
            pltpu.VMEM((rec_count, ext, width), BF16),
            pltpu.VMEM((rec_count, ext, width), BF16),
            pltpu.VMEM((rec_count, bank, width), BF16),
            pltpu.VMEM((rec_count, bank, width), BF16),
            pltpu.VMEM((rec_count, bank, width), BF16),
            pltpu.VMEM((rec_count * pairs * 16, width), BF16),
            pltpu.VMEM((rec_count, own + CONV, width), BF16),
            pltpu.VMEM((rec_count, pairs * 8, width), F32),
            pltpu.VMEM((2, group, keys), F32),
            pltpu.VMEM((2, keys, width), BF16),
            pltpu.VMEM((2, width // 128, keys, 256), BF16),
            pltpu.VMEM((6, width, half), BF16),
            pltpu.VMEM((2, half, width), BF16),
            pltpu.SemaphoreType.DMA((rec_count, 3)),
            pltpu.SemaphoreType.DMA((blocks,)),
            pltpu.SemaphoreType.DMA((8,)),
            pltpu.SemaphoreType.DMA((rec_count,)),
        ],
        compiler_params=pltpu.CompilerParams(vmem_limit_bytes=67043328),
        cost_estimate=pl.CostEstimate(
            flops=10 * 2 * rows * width * half,
            bytes_accessed=8 << 20,
            transcendentals=rows * 2048,
        ),
        name="attend",
    )(lengths, frames, halo, *memory, w_query, wq, w_key, wk, w_value, wv, w_out, wo, gain_first)
    others = swapped(vectors)
    output = pl.pallas_call(
        convolution_kernel,
        out_shape=jax.ShapeDtypeStruct((rec_count, own, width), BF16),
        in_specs=[smem] + [hbm] * 15 + vmem(2),
        out_specs=hbm,
        scratch_shapes=[
            pltpu.VMEM((rec_count, own + CONV, width), BF16),
            pltpu.VMEM((rec_count, own + CONV, width), BF16),
            pltpu.VMEM((rec_count, own + CONV, width), F32),
            pltpu.VMEM((rec_count, width // 128, own + CONV, 128), F32),
            pltpu.VMEM((8, chunk + 24, 128), BF16),
            pltpu.VMEM((width // 128, own, 128), BF16),
            pltpu.VMEM((own, width), BF16),
            pltpu.VMEM((own, width), F32),
            pltpu.VMEM((hidden_half // 128, own, 256), BF16),
            pltpu.VMEM((rec_count, own, width), BF16),
            pltpu.VMEM((2, half, width), BF16),
            pltpu.VMEM((2, 2, width, half), BF16),
            pltpu.VMEM((width // 128, CK, 128), BF16),
            pltpu.VMEM((2, half, width), BF16),
            pltpu.VMEM((hidden_half // 128, width, 256), BF16),
            pltpu.VMEM((hidden_half // 128, width, 256), BF16),
            pltpu.SemaphoreType.DMA((rec_count, 4)),
            pltpu.SemaphoreType.DMA((6 + width // 128 + hidden_half // 64,)),
            pltpu.SemaphoreType.DMA((chunks,)),
        ],
        compiler_params=pltpu.CompilerParams(vmem_limit_bytes=65200 << 10),
        cost_estimate=pl.CostEstimate(
            flops=22 * 2 * rows * width * half,
            bytes_accessed=16 << 20,
            transcendentals=rows * 2560,
        ),
        name="rest",
    )(
        lengths,
        frames,
        halo,
        ctx,
        w_out,
        wo,
        w_conv_in,
        wc,
        w_depth,
        wd,
        w_conv_out,
        wco,
        w_ffn_in,
        wi,
        w_ffn_out,
        wf,
        gain_conv.reshape(1, width),
        gain_ffn.reshape(1, width),
    )
    memory_out = vectors + others
    return (output, memory_out)


def solution(mesh):
    placed = (
        P(("groups", "rec"), "tm", None),
        P(("groups", "rec")),
        P(("groups", "rec"), "tm", None),
        P(),
        P(None, "mp"),
        P(None, "mp"),
        P(None, "mp"),
        P("mp", None),
        P(),
        P(None, None, "mp"),
        P(None, "mp"),
        P("mp", None),
        P(),
        P(None, "mp"),
        P(None, "mp"),
    )
    return jax.shard_map(
        on_device,
        mesh=mesh,
        in_specs=placed,
        out_specs=(P(("groups", "rec"), ("tm", "mp"), None), P(("groups", "rec"), "tm", None)),
        check_vma=False,
    )
```
